32 devices in a mesh: ctx: 8 (over z, x), tp: 4 (over y, core).
Axes of the slice: x: 2, y: 2, z: 4, core: 2. Of those that a mesh axis runs over, the one named last changes fastest.
Arguments:
- q_nope: bfloat16 [8, 128, 128], P('ctx', 'tp'), may hold values from -6 to 6
- q_rope: bfloat16 [8, 128, 64], P('ctx', 'tp'), may hold values from -256 to 256
- w_uk: bfloat16 [128, 128, 512], P('tp'), may hold values from -0.5 to 0.5
- w_uv: bfloat16 [128, 512, 128], P('tp'), may hold values from -3 to 3
- w_out: bfloat16 [16384, 7168], P('tp', 'ctx'), may hold values from -0.046875 to 0.046875
- prefix_cache: bfloat16 [32768, 576], P('ctx'), may hold values from -6 to 6
- block_table: int32 [512], P('ctx'), may hold values from 0 to 511, each once
- prefix_len: int32 [8], replicated, may hold values from 8192 to 32768
- suffix_cache: bfloat16 [8, 256, 576], P('ctx'), may hold values from -12 to 12
- suffix_len: int32 [8], P('ctx'), may hold values from 2 to 256
Outputs:
- layer_out: bfloat16 [8, 7168], P('tp', 'ctx')
The draws below stay inside these ranges and needn't reach their ends.
Inputs may be any that keep to these rules, and one draw needn't show every extreme that they name: A permutation: slots b * 64 to b * 64 + 63 of prefix_cache hold prefix positions block_table[b] * 64 onwards.
All inputs are finite; a program needn't handle non-finite values.
Results may differ from the reference program's by a relative error of at most 0.0078.
Values may be sent and summed in bfloat16 or wider, within the bound.
A program may use at most 64 MiB of HBM per device.

```python
import jax
import jax.numpy as jnp
from jax import lax

H = 128
LAT = 512
ROPE = 64
NOPE = 128
VDIM = 128
D = 7168
TOK_DEV = 4096
BLOCK = 64
SUF = 256
REQUESTS = 8
NPRE = 32768
NBLK = 512
N_CTX = 8


def shared_base(key):
    return jax.random.normal(jax.random.fold_in(key, 11), (REQUESTS, ROPE), jnp.float32)


def suffix_rope_part(key):
    noise = jax.random.normal(jax.random.fold_in(key, 13), (REQUESTS, SUF, ROPE), jnp.float32)
    return shared_base(key)[:, None, :] + noise


def draw_suffix_cache(key, part):
    latent = jax.random.normal(jax.random.fold_in(key, 12), (REQUESTS, SUF, LAT), jnp.float32)
    rope = suffix_rope_part(key)
    return jnp.clip(jnp.concatenate([latent, rope], axis=2), -12.0, 12.0).astype(jnp.bfloat16)


def draw_q_rope(key, part):
    noise = jax.random.normal(jax.random.fold_in(key, 21), (REQUESTS, H, ROPE), jnp.float32)
    query = shared_base(key)[:, None, :] + noise
    return jnp.clip(query, -256.0, 256.0).astype(jnp.bfloat16)


def set_ends(drawn, stream_key, low, top_value):
    longest = drawn.shape.index(max(drawn.shape))
    spots = []
    for shift in (0, 1):
        where = [jax.random.randint(jax.random.fold_in(stream_key, axis), (), 0, length) for axis, length in enumerate(drawn.shape)]
        where[longest] = (where[longest] + shift) % drawn.shape[longest]
        spots.append(tuple(where))
    return drawn.at[spots[0]].set(low).at[spots[1]].set(top_value)


def block_scale(stream_key, dims, split, low, high):
    def one(axis_at, blocks):
        steps = jax.random.uniform(jax.random.fold_in(jax.random.fold_in(stream_key, 6), axis_at), (blocks,), jnp.float32, low / len(split), high / len(split))
        return jnp.repeat(jnp.exp(steps), dims[axis_at] // blocks).reshape((-1,) + (1,) * (len(dims) - axis_at - 1))

    level = one(*split[0])
    for cut in split[1:]:
        level = level * one(*cut)
    return level


def normal_values(own_key, shape, scale, bound, split=(), held_as=jnp.bfloat16):
    entries = scale * jax.random.normal(own_key, shape, jnp.float32)
    if split:
        entries = entries * block_scale(own_key, shape, split, -0.22, 0.18)
    return jnp.clip(entries, -bound, bound).astype(held_as)


def setup_inputs(seed: int = 0) -> dict:
    streams_of = jax.random.split(jax.random.key(seed), 11)
    q_nope = normal_values(streams_of[0], (REQUESTS, H, NOPE), 1.0, 6.0, ((0, 8), (1, 4)))
    q_rope = draw_q_rope(jax.random.fold_in(streams_of[10], 71), 0)
    w_uk = normal_values(streams_of[2], (H, NOPE, LAT), NOPE ** -0.5, 0.5, ((0, 4),))
    w_uv = normal_values(streams_of[3], (H, LAT, VDIM), 0.5, 3.0, ((0, 4),))
    w_out = normal_values(streams_of[4], (H * VDIM, D), (H * VDIM) ** -0.5, 0.046875, ((0, 4), (1, 8)))
    prefix_cache = normal_values(streams_of[5], (NPRE, LAT + ROPE), 1.0, 6.0, ((0, 8),))
    block_table = jax.random.permutation(streams_of[6], NBLK).astype(jnp.int32)
    prefix_len = set_ends(jax.random.randint(streams_of[7], (REQUESTS,), NPRE // 4, NPRE + 1), jax.random.fold_in(streams_of[7], 1), NPRE // 4, NPRE).astype(jnp.int32)
    suffix_cache = draw_suffix_cache(jax.random.fold_in(streams_of[10], 71), 0)
    suffix_len = set_ends(jax.random.randint(streams_of[9], (REQUESTS,), 2, SUF + 1), jax.random.fold_in(streams_of[9], 1), 2, SUF).astype(jnp.int32)
    return {"q_nope": q_nope, "q_rope": q_rope, "w_uk": w_uk, "w_uv": w_uv, "w_out": w_out, "prefix_cache": prefix_cache, "block_table": block_table, "prefix_len": prefix_len, "suffix_cache": suffix_cache, "suffix_len": suffix_len}


masked_value = -1e30


def summarize(scores, visible, values, pattern):
    row_peak = jnp.max(jnp.where(visible, scores, masked_value), axis=2)
    weights = jnp.where(visible, jnp.exp(scores - row_peak[:, :, None]), 0.0).astype(jnp.bfloat16)
    weights = lax.optimization_barrier(weights).astype(jnp.float32)
    return row_peak, jnp.sum(weights, axis=2), jnp.einsum(pattern, weights, values)


def reference(q_nope, q_rope, w_uk, w_uv, w_out, prefix_cache, block_table, prefix_len, suffix_cache, suffix_len):
    softmax_scale = (NOPE + ROPE) ** -0.5
    q_latent = jnp.einsum("rhn,hnc->rhc", q_nope.astype(jnp.float32), w_uk.astype(jnp.float32)).astype(jnp.bfloat16)
    joined = lax.optimization_barrier(jnp.concatenate([q_latent, q_rope], axis=2)).astype(jnp.float32)
    positions = (block_table[:, None] * BLOCK + jnp.arange(BLOCK, dtype=jnp.int32)[None, :]).reshape(N_CTX, TOK_DEV)
    segments = prefix_cache.reshape(N_CTX, TOK_DEV, LAT + ROPE)

    def segment_part(pieces):
        block_cache, block_positions = pieces
        cache_wide = block_cache.astype(jnp.float32)
        scores = jnp.einsum("rhc,tc->rht", joined, cache_wide) * softmax_scale
        visible = (block_positions[None, :] < prefix_len[:, None])[:, None, :]
        return summarize(scores, visible, cache_wide[:, :LAT], "rht,tc->rhc")

    seg_peak, seg_mass, seg_weighted = lax.map(segment_part, (segments, positions))
    suffix_wide = suffix_cache.astype(jnp.float32)
    suffix_scores = jnp.einsum("rhc,rtc->rht", joined, suffix_wide) * softmax_scale
    suffix_slots = jnp.arange(SUF, dtype=jnp.int32)
    suffix_visible = (suffix_slots[None, :] < suffix_len[:, None])[:, None, :]
    tail_peak, tail_mass, tail_weighted = summarize(suffix_scores, suffix_visible, suffix_wide[:, :, :LAT], "rht,rtc->rhc")
    highest = jnp.maximum(jnp.max(seg_peak, axis=0), tail_peak)
    factors = jnp.exp(seg_peak - highest[None])
    tail_factor = jnp.exp(tail_peak - highest)
    total_mass = jnp.sum(factors * seg_mass, axis=0) + tail_factor * tail_mass
    total_weighted = jnp.sum(factors[..., None] * seg_weighted, axis=0) + tail_factor[:, :, None] * tail_weighted
    attention = total_weighted / total_mass[:, :, None]
    head_values = jnp.einsum("rhc,hcv->rhv", attention, w_uv.astype(jnp.float32), precision=lax.Precision.HIGHEST).astype(jnp.bfloat16)
    flat_values = head_values.reshape(REQUESTS, H * VDIM)
    return jnp.dot(flat_values, w_out, preferred_element_type=jnp.float32).astype(jnp.bfloat16)
```

```python
import functools

import jax
import jax.numpy as jnp
from jax import lax
from jax.experimental import pallas as pl
from jax.experimental.pallas import tpu as pltpu
from jax.sharding import PartitionSpec as P

LAT = 512
ROPE = 64
NOPE = 128
BLOCK = 64
LANES = 128
MASKED = -1e30
FLOOR = -1e29
LOG2E = 1.4426950408889634
MESH = pl.DeviceIdType.MESH


def mergers_of(n):
    return (n // 2, n // 4) if n % 4 == 0 else (n, 0)


def flipped(index, k):
    bit = 1
    out = index
    while bit <= k:
        if k & bit:
            out = out + bit * (1 - 2 * lax.rem(index // bit, 2))
        bit *= 2
    return out


def kernel(
    sizes,
    suffix_len_hbm,
    table_hbm,
    prefix_len_hbm,
    q_nope_hbm,
    q_rope_hbm,
    w_uk_hbm,
    w_uv_hbm,
    w_out_hbm,
    prefix_hbm,
    suffix_hbm,
    out_ref,
    q_rope_ref,
    q_pack,
    q_all,
    qn_rows,
    qr_rows,
    query,
    w_uk,
    w_uv,
    w_out,
    cache,
    mask,
    scores,
    peak,
    mass,
    weighted,
    inverse,
    msg,
    got,
    stat_msg,
    stat_got,
    stat_rows,
    stat_columns,
    hv_all,
    part,
    part_got,
    table_ref,
    prefix_len_ref,
    suffix_len_ref,
    load_sem,
    small_sem,
    q_send,
    q_recv,
    m_send,
    m_recv,
    s_send,
    s_recv,
    h_send,
    h_recv,
    p_send,
    p_recv,
):
    n, t, own, heads, requests, tokens, suffix = sizes
    rows = requests * heads
    vdim = w_uv.shape[2]
    mergers, first = mergers_of(n)
    merge_heads = heads // mergers
    merge_rows = merge_heads * requests
    me = lax.axis_index("ctx")
    me_tp = lax.axis_index("tp")
    half_heads = heads // 2

    def ctx(index):
        return (index, me_tp)

    def copy_to(src, dst, send, recv, device):
        return pltpu.make_async_remote_copy(
            src_ref=src,
            dst_ref=dst,
            send_sem=send,
            recv_sem=recv,
            device_id=device,
            device_id_type=MESH,
        )

    smalls = [
        pltpu.make_async_copy(src, dst, small_sem.at[i])
        for i, (src, dst) in enumerate(
            (
                (q_nope_hbm, q_pack.at[:, pl.ds(0, heads)]),
                (q_rope_hbm, q_rope_ref),
                (table_hbm, table_ref),
                (prefix_len_hbm, prefix_len_ref),
                (suffix_len_hbm, suffix_len_ref),
            )
        )
    ]
    for small in smalls:
        small.start()
    loads = [
        pltpu.make_async_copy(w_uk_hbm, w_uk, load_sem.at[0]),
        pltpu.make_async_copy(prefix_hbm, cache.at[:, pl.ds(0, tokens)], load_sem.at[1]),
    ]
    for o in range(own):
        loads.append(
            pltpu.make_async_copy(
                suffix_hbm.at[o],
                cache.at[:, pl.ds(tokens + o * suffix, suffix)],
                load_sem.at[4 + o],
            )
        )
    uv_load = pltpu.make_async_copy(w_uv_hbm, w_uv, load_sem.at[2])
    out_load = pltpu.make_async_copy(w_out_hbm, w_out, load_sem.at[3])
    barrier = pltpu.get_barrier_semaphore()
    for k in reversed(range(1, n)):
        pl.semaphore_signal(barrier, inc=1, device_id=ctx(flipped(me, k)), device_id_type=MESH)
    for k in reversed(range(1, t)):
        pl.semaphore_signal(
            barrier, inc=1, device_id=(me, flipped(me_tp, k)), device_id_type=MESH
        )
    for small in smalls[:2]:
        small.wait()
    for o in range(own):
        rope = q_rope_ref[o]
        q_pack[o, heads : heads + half_heads, :] = jnp.concatenate(
            [rope[:half_heads], rope[half_heads:]], axis=1
        )
    for load in loads:
        load.start()
    uv_load.start()
    out_load.start()
    pl.semaphore_wait(barrier, n - 1 + t - 1)

    mine = pl.ds(me * own, own)
    q_copies = []
    for k in reversed(range(1, n)):
        copy = copy_to(q_pack, q_all.at[mine], q_send.at[k], q_recv.at[k], ctx(flipped(me, k)))
        copy.start()
        q_copies.append(copy)
    q_all[mine] = q_pack[...]
    for small in smalls[2:]:
        small.wait()

    stat_rows[...] = jnp.zeros_like(stat_rows)
    row = lax.broadcasted_iota(jnp.int32, (requests, LANES), 0)
    lane = lax.broadcasted_iota(jnp.int32, (requests, LANES), 1)
    limit = jnp.zeros((requests, LANES), jnp.int32)
    for r in range(requests):
        limit = jnp.where(row == r, prefix_len_ref[r], limit)
    per_tile = LANES // BLOCK
    for i in range(tokens // LANES):
        position = lane + table_ref[i * per_tile] * BLOCK
        for j in range(1, per_tile):
            moved = lane + (table_ref[i * per_tile + j] * BLOCK - j * BLOCK)
            position = jnp.where(lane >= j * BLOCK, moved, position)
        mask[:, i * LANES : (i + 1) * LANES] = jnp.where(position < limit, 0.0, MASKED)
    for o in range(own):
        for i in range(suffix // LANES):
            slot = lane + i * LANES
            start = tokens + o * suffix + i * LANES
            seen = (slot < suffix_len_ref[o]) & (row == me * own + o)
            mask[:, start : start + LANES] = jnp.where(seen, 0.0, MASKED)

    for copy in q_copies:
        copy.wait()
    for r in range(requests):
        qn_rows[pl.ds(r, heads, stride=requests), :] = q_all[r, :heads, :].astype(jnp.float32)
        rope = q_all[r, heads : heads + half_heads, :].astype(jnp.float32)
        qr_rows[pl.ds(r, half_heads, stride=requests), :] = rope[:, :ROPE]
        qr_rows[pl.ds(half_heads * requests + r, half_heads, stride=requests), :] = rope[:, ROPE:]
    query[:, LAT:] = qr_rows[...].astype(jnp.bfloat16)
    loads[0].wait()
    latents = []
    for h in range(heads):
        q = qn_rows[h * requests : (h + 1) * requests, :]
        latents.append(
            jnp.dot(q.astype(jnp.bfloat16), w_uk[h], preferred_element_type=jnp.float32)
        )
    query[:, :LAT] = jnp.concatenate(latents, axis=0).astype(jnp.bfloat16)

    scale = LOG2E * (NOPE + ROPE) ** (-0.5)
    spans = [(0, tokens)] + [(tokens + o * suffix, suffix) for o in range(own)]
    for load in loads[1:]:
        load.wait()
    for i, (start, length) in enumerate(spans):
        s = jnp.dot(
            query[...], cache[:, start : start + length], preferred_element_type=jnp.float32
        )
        s = (s * scale).reshape(heads, requests, length)
        s = (s + mask[:, start : start + length][None]).reshape(rows, length)
        scores[:, start : start + length] = s
        top = s[:, :LANES]
        for j in range(1, length // LANES):
            top = jnp.maximum(top, s[:, j * LANES : (j + 1) * LANES])
        peak[...] = top if i == 0 else jnp.maximum(peak[...], top)
    highest = jnp.maximum(jnp.max(peak[...], axis=1, keepdims=True), FLOOR)
    peak[...] = jnp.broadcast_to(highest, (rows, LANES))
    for i, (start, length) in enumerate(spans):
        p = jnp.exp2(scores[:, start : start + length] - peak[:, :1]).astype(jnp.bfloat16)
        wide = p.astype(jnp.float32)
        total = wide[:, :LANES]
        for j in range(1, length // LANES):
            total = total + wide[:, j * LANES : (j + 1) * LANES]
        mass[...] = total if i == 0 else mass[...] + total
        term = lax.dot_general(
            p,
            cache[:LAT, start : start + length],
            (((1,), (1,)), ((), ())),
            preferred_element_type=jnp.float32,
        )
        weighted[...] = term if i == 0 else weighted[...] + term
    sums = jnp.broadcast_to(jnp.sum(mass[...], axis=1, keepdims=True), (rows, LANES))
    some = sums > 0.0
    safe = jnp.where(some, sums, 1.0)
    inverse[...] = jnp.where(some, 1.0 / safe, 0.0)
    level = jnp.where(some, peak[...] + jnp.log2(safe), MASKED)
    level_row = jnp.transpose(level)[:1]
    for j in range(mergers):
        stat_msg[j] = level_row[:, j * merge_rows : (j + 1) * merge_rows]

    nearest = (me // (n // 2)) * (mergers // 2) + lax.rem(me, mergers // 2)
    merging = jnp.logical_and(me >= first, me < first + mergers)
    order = [flipped(nearest, k) for k in range(mergers)]

    def stat_copy(k):
        j = order[k]
        return copy_to(stat_msg.at[j], stat_got.at[me], s_send.at[k], s_recv.at[me], ctx(first + j))

    def sum_copy(k):
        j = order[k]
        return copy_to(msg.at[j], got.at[me], m_send.at[k], m_recv.at[me], ctx(first + j))

    for k in reversed(range(1, mergers)):
        stat_copy(k).start()

    @pl.when(jnp.logical_not(merging))
    def _():
        stat_copy(0).start()

    uv_load.wait()
    for k in reversed(range(mergers)):
        j = order[k]
        for i in range(merge_heads):
            at = pl.multiple_of((j * merge_heads + i) * requests, requests)
            x = weighted[pl.ds(at, requests), :]
            high = x.astype(jnp.bfloat16).astype(jnp.float32)
            pieces = jnp.concatenate([high, x - high], axis=0).astype(jnp.bfloat16)
            y = jnp.dot(
                pieces, w_uv[j * merge_heads + i], preferred_element_type=jnp.float32
            )
            y = (y[:requests] + y[requests:]) * inverse[pl.ds(at, requests), :vdim]
            qn_rows[i * requests : (i + 1) * requests, :] = y
        msg[j] = qn_rows[:merge_rows, :].astype(jnp.bfloat16)
        if k > 0:
            sum_copy(k).start()

    @pl.when(jnp.logical_not(merging))
    def _():
        sum_copy(0).start()

    def value_copy(k):
        at = hv_all.at[me - first]
        return copy_to(at, at, h_send.at[k], h_recv.at[me - first], ctx(flipped(me, k)))

    @pl.when(merging)
    def _():
        got[me] = msg[me - first]
        stat_got[me] = stat_msg[me - first]
        for k in range(1, n):
            source = flipped(me, k)
            copy_to(
                stat_msg.at[0],
                stat_got.at[source],
                s_send.at[0],
                s_recv.at[source],
                ctx(source),
            ).wait_recv()
        for k in range(n):
            stat_rows[k : k + 1, :merge_rows] = stat_got[k]
        levels = stat_rows[:n, :]
        share_of = jnp.exp2(levels - jnp.max(levels, axis=0, keepdims=True))
        stat_rows[:n, :] = share_of / jnp.sum(share_of, axis=0, keepdims=True)
        stat_columns[...] = jnp.transpose(stat_rows[...])
        for k in range(1, n):
            source = flipped(me, k)
            copy_to(
                msg.at[0], got.at[source], m_send.at[0], m_recv.at[source], ctx(source)
            ).wait_recv()
        merged = None
        for k in range(n):
            term = stat_columns[:merge_rows, k : k + 1] * got[k].astype(jnp.float32)
            merged = term if merged is None else merged + term
        values = [merged[i * requests : (i + 1) * requests] for i in range(merge_heads)]
        hv_all[me - first] = jnp.concatenate(values, axis=1).astype(jnp.bfloat16)
        for k in reversed(range(1, n)):
            value_copy(k).start()

    out_load.wait()
    depth = merge_heads * vdim
    total = None
    for k in range(mergers):
        j = order[k]

        def arrived():
            copy_to(
                hv_all.at[j], hv_all.at[j], h_send.at[0], h_recv.at[j], ctx(first + j)
            ).wait_recv()

        if k == 0:
            pl.when(jnp.logical_not(merging))(arrived)
        else:
            arrived()
        term = jnp.dot(
            hv_all[j],
            w_out[pl.ds(pl.multiple_of(j * depth, depth), depth), :],
            preferred_element_type=jnp.float32,
        )
        total = term if total is None else total + term
    share = requests // t
    for i in range(t):
        part[i] = total[i * share : (i + 1) * share]
    p_copies = []
    for k in reversed(range(1, t)):
        to = flipped(me_tp, k)
        copy = copy_to(part.at[to], part_got.at[k], p_send.at[k], p_recv.at[k], (me, to))
        copy.start()
        p_copies.append((k, copy))
    for k in range(1, mergers):
        stat_copy(k).wait_send()
        sum_copy(k).wait_send()

    @pl.when(jnp.logical_not(merging))
    def _():
        stat_copy(0).wait_send()
        sum_copy(0).wait_send()

    @pl.when(merging)
    def _():
        for k in range(1, n):
            value_copy(k).wait_send()

    result = part[me_tp]
    for k, copy in p_copies[::-1]:
        copy.wait()
        result = result + part_got[k]
    out_ref[...] = result.astype(jnp.bfloat16)


def on_device(
    n,
    t,
    q_nope,
    q_rope,
    w_uk,
    w_uv,
    w_out,
    prefix_cache,
    block_table,
    prefix_len,
    suffix_cache,
    suffix_len,
):
    own, heads, _ = q_nope.shape
    requests = own * n
    tokens, width = prefix_cache.shape
    suffix = suffix_cache.shape[1]
    slots = tokens + own * suffix
    rows = requests * heads
    mergers, _ = mergers_of(n)
    merge_heads = heads // mergers
    merge_rows = merge_heads * requests
    pack_rows = heads + max(16, heads // 2)
    vdim = w_uv.shape[2]
    columns = w_out.shape[1]
    share = requests // t
    bf, f32 = jnp.bfloat16, jnp.float32
    sizes = (n, t, own, heads, requests, tokens, suffix)
    vmem = pl.BlockSpec(memory_space=pltpu.VMEM)
    hbm = pl.BlockSpec(memory_space=pl.ANY)
    dma = pltpu.SemaphoreType.DMA
    return pl.pallas_call(
        functools.partial(kernel, sizes),
        out_shape=jax.ShapeDtypeStruct((share, columns), bf),
        in_specs=[hbm] * 10,
        out_specs=vmem,
        scratch_shapes=[
            pltpu.VMEM((own, heads, ROPE), bf),
            pltpu.VMEM((own, pack_rows, LANES), bf),
            pltpu.VMEM((requests, pack_rows, LANES), bf),
            pltpu.VMEM((rows, NOPE), f32),
            pltpu.VMEM((rows, ROPE), f32),
            pltpu.VMEM((rows, width), bf),
            pltpu.VMEM(w_uk.shape, bf),
            pltpu.VMEM(w_uv.shape, bf),
            pltpu.VMEM(w_out.shape, bf),
            pltpu.VMEM((width, slots), bf),
            pltpu.VMEM((requests, slots), f32),
            pltpu.VMEM((rows, slots), f32),
            pltpu.VMEM((rows, LANES), f32),
            pltpu.VMEM((rows, LANES), f32),
            pltpu.VMEM((rows, LAT), f32),
            pltpu.VMEM((rows, LANES), f32),
            pltpu.VMEM((mergers, merge_rows, vdim), bf),
            pltpu.VMEM((n, merge_rows, vdim), bf),
            pltpu.VMEM((mergers, 1, merge_rows), f32),
            pltpu.VMEM((n, 1, merge_rows), f32),
            pltpu.VMEM((LANES, LANES), f32),
            pltpu.VMEM((LANES, LANES), f32),
            pltpu.VMEM((mergers, requests, merge_heads * vdim), bf),
            pltpu.VMEM((t, share, columns), f32),
            pltpu.VMEM((t, share, columns), f32),
            pltpu.SMEM(block_table.shape, jnp.int32),
            pltpu.SMEM(prefix_len.shape, jnp.int32),
            pltpu.SMEM(suffix_len.shape, jnp.int32),
            dma((4 + own,)),
            dma((5,)),
            dma((n,)),
            dma((n,)),
            dma((mergers,)),
            dma((n,)),
            dma((mergers,)),
            dma((n,)),
            dma((n,)),
            dma((mergers,)),
            dma((t,)),
            dma((t,)),
        ],
        compiler_params=pltpu.CompilerParams(
            collective_id=0, has_side_effects=True, vmem_limit_bytes=60 * 1024 * 1024
        ),
    )(
        suffix_len,
        block_table,
        prefix_len,
        q_nope,
        q_rope,
        w_uk,
        w_uv,
        w_out,
        prefix_cache.T,
        jnp.swapaxes(suffix_cache, 1, 2),
    )


def solution(mesh):
    placed = (
        P("ctx", "tp", None),
        P("ctx", "tp", None),
        P("tp", None, None),
        P("tp", None, None),
        P("tp", "ctx"),
        P("ctx", None),
        P("ctx"),
        P(),
        P("ctx", None, None),
        P("ctx"),
    )
    return jax.shard_map(
        functools.partial(on_device, mesh.shape["ctx"], mesh.shape["tp"]),
        mesh=mesh,
        in_specs=placed,
        out_specs=P("tp", "ctx"),
        check_vma=False,
    )
```

```python
import functools

import jax
import jax.numpy as jnp
from jax import lax
from jax.experimental import pallas as pl
from jax.experimental.pallas import tpu as pltpu
from jax.sharding import PartitionSpec as P

LAT = 512
ROPE = 64
NOPE = 128
BLOCK = 64
LANES = 128
MASKED = -1e30
FLOOR = -1e29
LOG2E = 1.4426950408889634
MESH = pl.DeviceIdType.MESH


def mergers_of(n):
    return (n // 2, n // 4) if n % 4 == 0 else (n, 0)


def flipped(index, k):
    bit = 1
    out = index
    while bit <= k:
        if k & bit:
            out = out + bit * (1 - 2 * lax.rem(index // bit, 2))
        bit *= 2
    return out


def kernel(
    sizes,
    suffix_len_hbm,
    table_hbm,
    prefix_len_hbm,
    q_nope_hbm,
    q_rope_hbm,
    w_uk_hbm,
    w_uv_hbm,
    w_out_hbm,
    prefix_hbm,
    suffix_hbm,
    out_ref,
    q_rope_ref,
    q_pack,
    q_all,
    qn_rows,
    qr_rows,
    query,
    w_uk,
    w_uv,
    w_out,
    cache,
    mask,
    scores,
    peak,
    mass,
    weighted,
    msg,
    got,
    stat_msg,
    stat_got,
    stat_rows,
    stat_columns,
    hv_all,
    part,
    part_got,
    table_ref,
    prefix_len_ref,
    suffix_len_ref,
    load_sem,
    small_sem,
    q_send,
    q_recv,
    m_send,
    m_recv,
    s_send,
    s_recv,
    h_send,
    h_recv,
    p_send,
    p_recv,
):
    n, t, own, heads, requests, tokens, suffix = sizes
    rows = requests * heads
    vdim = w_uv.shape[2]
    mergers, first = mergers_of(n)
    merge_heads = heads // mergers
    merge_rows = merge_heads * requests
    me = lax.axis_index("ctx")
    me_tp = lax.axis_index("tp")
    half_heads = heads // 2

    def ctx(index):
        return (index, me_tp)

    def copy_to(src, dst, send, recv, device):
        return pltpu.make_async_remote_copy(
            src_ref=src,
            dst_ref=dst,
            send_sem=send,
            recv_sem=recv,
            device_id=device,
            device_id_type=MESH,
        )

    smalls = [
        pltpu.make_async_copy(src, dst, small_sem.at[i])
        for i, (src, dst) in enumerate(
            (
                (q_nope_hbm, q_pack.at[:, pl.ds(0, heads)]),
                (q_rope_hbm, q_rope_ref),
                (table_hbm, table_ref),
                (prefix_len_hbm, prefix_len_ref),
                (suffix_len_hbm, suffix_len_ref),
            )
        )
    ]
    for small in smalls:
        small.start()
    loads = [
        pltpu.make_async_copy(w_uk_hbm, w_uk, load_sem.at[0]),
        pltpu.make_async_copy(prefix_hbm, cache.at[:, pl.ds(0, tokens)], load_sem.at[1]),
    ]
    for o in range(own):
        loads.append(
            pltpu.make_async_copy(
                suffix_hbm.at[o],
                cache.at[:, pl.ds(tokens + o * suffix, suffix)],
                load_sem.at[4 + o],
            )
        )
    uv_load = pltpu.make_async_copy(w_uv_hbm, w_uv, load_sem.at[2])
    out_load = pltpu.make_async_copy(w_out_hbm, w_out, load_sem.at[3])
    barrier = pltpu.get_barrier_semaphore()
    for k in reversed(range(1, n)):
        pl.semaphore_signal(barrier, inc=1, device_id=ctx(flipped(me, k)), device_id_type=MESH)
    for k in reversed(range(1, t)):
        pl.semaphore_signal(
            barrier, inc=1, device_id=(me, flipped(me_tp, k)), device_id_type=MESH
        )
    for small in smalls[:2]:
        small.wait()
    for o in range(own):
        rope = q_rope_ref[o]
        q_pack[o, heads : heads + half_heads, :] = jnp.concatenate(
            [rope[:half_heads], rope[half_heads:]], axis=1
        )
    for load in loads:
        load.start()
    uv_load.start()
    out_load.start()
    pl.semaphore_wait(barrier, n - 1 + t - 1)

    mine = pl.ds(me * own, own)
    q_copies = []
    for k in reversed(range(1, n)):
        copy = copy_to(q_pack, q_all.at[mine], q_send.at[k], q_recv, ctx(flipped(me, k)))
        copy.start()
        q_copies.append(copy)
    q_all[mine] = q_pack[...]
    for small in smalls[2:]:
        small.wait()

    stat_rows[...] = jnp.zeros_like(stat_rows)
    row = lax.broadcasted_iota(jnp.int32, (requests, LANES), 0)
    lane = lax.broadcasted_iota(jnp.int32, (requests, LANES), 1)
    limit = jnp.zeros((requests, LANES), jnp.int32)
    for r in range(requests):
        limit = jnp.where(row == r, prefix_len_ref[r], limit)
    per_tile = LANES // BLOCK
    for i in range(tokens // LANES):
        position = lane + table_ref[i * per_tile] * BLOCK
        for j in range(1, per_tile):
            moved = lane + (table_ref[i * per_tile + j] * BLOCK - j * BLOCK)
            position = jnp.where(lane >= j * BLOCK, moved, position)
        mask[:, i * LANES : (i + 1) * LANES] = jnp.where(position < limit, 0.0, MASKED)
    for o in range(own):
        for i in range(suffix // LANES):
            slot = lane + i * LANES
            start = tokens + o * suffix + i * LANES
            seen = (slot < suffix_len_ref[o]) & (row == me * own + o)
            mask[:, start : start + LANES] = jnp.where(seen, 0.0, MASKED)

    others = q_all.at[pl.ds(0, (n - 1) * own)]
    pltpu.make_async_copy(others, others, q_recv).wait()
    for r in range(requests):
        qn_rows[pl.ds(r, heads, stride=requests), :] = q_all[r, :heads, :].astype(jnp.float32)
        rope = q_all[r, heads : heads + half_heads, :].astype(jnp.float32)
        qr_rows[pl.ds(r, half_heads, stride=requests), :] = rope[:, :ROPE]
        qr_rows[pl.ds(half_heads * requests + r, half_heads, stride=requests), :] = rope[:, ROPE:]
    query[:, LAT:] = qr_rows[...].astype(jnp.bfloat16)
    loads[0].wait()
    latents = []
    for h in range(heads):
        q = qn_rows[h * requests : (h + 1) * requests, :]
        latents.append(
            jnp.dot(q.astype(jnp.bfloat16), w_uk[h], preferred_element_type=jnp.float32)
        )
    query[:, :LAT] = jnp.concatenate(latents, axis=0).astype(jnp.bfloat16)

    scale = LOG2E * (NOPE + ROPE) ** (-0.5)
    spans = [(0, tokens)] + [(tokens + o * suffix, suffix) for o in range(own)]
    for load in loads[1:]:
        load.wait()
    uv_load.wait()
    block = rows // 2
    for b in range(2):
        at = slice(b * block, (b + 1) * block)
        tops = []
        for start, length in spans:
            s = jnp.dot(
                query[at, :], cache[:, start : start + length], preferred_element_type=jnp.float32
            )
            s = (s * scale).reshape(heads // 2, requests, length)
            s = (s + mask[:, start : start + length][None]).reshape(block, length)
            scores[at, start : start + length] = s
            tops += [s[:, j * LANES : (j + 1) * LANES] for j in range(length // LANES)]
        top = functools.reduce(jnp.maximum, tops)
        highest = jnp.maximum(jnp.max(top, axis=1, keepdims=True), FLOOR)
        peak[at, :] = jnp.broadcast_to(highest, (block, LANES))
    for i, (start, length) in enumerate(spans):
        p = jnp.exp2(scores[:, start : start + length] - peak[:, :1]).astype(jnp.bfloat16)
        wide = p.astype(jnp.float32)
        total = wide[:, :LANES]
        for j in range(1, length // LANES):
            total = total + wide[:, j * LANES : (j + 1) * LANES]
        mass[...] = total if i == 0 else mass[...] + total
        term = lax.dot_general(
            p,
            cache[:LAT, start : start + length],
            (((1,), (1,)), ((), ())),
            preferred_element_type=jnp.float32,
        )
        weighted[...] = term if i == 0 else weighted[...] + term
    stat_at = lax.broadcasted_iota(jnp.int32, (2, rows), 0)
    mass_row = jnp.sum(jnp.transpose(mass[...]), axis=0, keepdims=True)
    peak_row = jnp.transpose(peak[...])[:1]
    stats = jnp.where(stat_at == 0, peak_row, mass_row)
    for j in range(mergers):
        stat_msg[j] = stats[:, j * merge_rows : (j + 1) * merge_rows]

    nearest = (me // (n // 2)) * (mergers // 2) + lax.rem(me, mergers // 2)
    merging = jnp.logical_and(me >= first, me < first + mergers)
    order = [flipped(nearest, k) for k in range(mergers)]

    def stat_copy(k):
        j = order[k]
        return copy_to(stat_msg.at[j], stat_got.at[me], s_send.at[k], s_recv, ctx(first + j))

    def sum_copy(k):
        j = order[k]
        return copy_to(msg.at[j], got.at[me], m_send.at[k], m_recv, ctx(first + j))

    for k in reversed(range(1, mergers)):
        stat_copy(k).start()

    @pl.when(jnp.logical_not(merging))
    def _():
        stat_copy(0).start()

    for k in reversed(range(mergers)):
        j = order[k]
        parts = []
        for i in range(merge_heads):
            at = pl.multiple_of((j * merge_heads + i) * requests, requests)
            x = weighted[pl.ds(at, requests), :]
            high = x.astype(jnp.bfloat16).astype(jnp.float32)
            pieces = jnp.concatenate([high, x - high], axis=0).astype(jnp.bfloat16)
            y = jnp.dot(
                pieces, w_uv[j * merge_heads + i], preferred_element_type=jnp.float32
            )
            parts.append(y[:requests] + y[requests:])
        msg[j] = jnp.concatenate(parts, axis=0).astype(jnp.bfloat16)
        if k > 0:
            sum_copy(k).start()

    @pl.when(jnp.logical_not(merging))
    def _():
        sum_copy(0).start()

    def value_copy(k):
        at = hv_all.at[me - first]
        to = k - 1 + (k - 1 + n - me) // n
        return copy_to(at, at, h_send.at[k], h_recv.at[me - first], ctx(to))

    @pl.when(merging)
    def _():
        got[me] = msg[me - first]
        stat_got[me] = stat_msg[me - first]
        others = stat_got.at[pl.ds(0, n - 1)]
        pltpu.make_async_copy(others, others, s_recv).wait()
        tops = jnp.concatenate([stat_got[k][:1] for k in range(n)], axis=0)
        masses = jnp.concatenate([stat_got[k][1:] for k in range(n)], axis=0)
        share_of = jnp.exp2(tops - jnp.max(tops, axis=0, keepdims=True))
        whole = jnp.sum(share_of * masses, axis=0, keepdims=True)
        stat_rows[:n, :merge_rows] = share_of / whole
        stat_columns[...] = jnp.transpose(stat_rows[...])
        others = got.at[pl.ds(0, n - 1)]
        pltpu.make_async_copy(others, others, m_recv).wait()
        merged = None
        for k in range(n):
            term = stat_columns[:merge_rows, k : k + 1] * got[k].astype(jnp.float32)
            merged = term if merged is None else merged + term
        values = [merged[i * requests : (i + 1) * requests] for i in range(merge_heads)]
        hv_all[me - first] = jnp.concatenate(values, axis=1).astype(jnp.bfloat16)
        for k in range(1, n):
            value_copy(k).start()

    out_load.wait()
    depth = merge_heads * vdim
    total = None
    for k in range(mergers):
        j = order[k]

        def arrived():
            copy_to(
                hv_all.at[j], hv_all.at[j], h_send.at[0], h_recv.at[j], ctx(first + j)
            ).wait_recv()

        if k == 0:
            pl.when(jnp.logical_not(merging))(arrived)
        else:
            arrived()
        term = jnp.dot(
            hv_all[j],
            w_out[pl.ds(pl.multiple_of(j * depth, depth), depth), :],
            preferred_element_type=jnp.float32,
        )
        total = term if total is None else total + term
    share = requests // t
    for i in range(t):
        part[i] = total[i * share : (i + 1) * share]
    p_copies = []
    for k in reversed(range(1, t)):
        to = flipped(me_tp, k)
        copy = copy_to(part.at[to], part_got.at[k], p_send.at[k], p_recv.at[k], (me, to))
        copy.start()
        p_copies.append((k, copy))
    for copy in q_copies:
        copy.wait_send()
    for k in range(1, mergers):
        stat_copy(k).wait_send()
        sum_copy(k).wait_send()

    @pl.when(jnp.logical_not(merging))
    def _():
        stat_copy(0).wait_send()
        sum_copy(0).wait_send()

    @pl.when(merging)
    def _():
        for k in range(1, n):
            value_copy(k).wait_send()

    result = part[me_tp]
    for k, copy in p_copies[::-1]:
        copy.wait()
        result = result + part_got[k]
    out_ref[...] = result.astype(jnp.bfloat16)


def on_device(
    n,
    t,
    q_nope,
    q_rope,
    w_uk,
    w_uv,
    w_out,
    prefix_cache,
    block_table,
    prefix_len,
    suffix_cache,
    suffix_len,
):
    own, heads, _ = q_nope.shape
    requests = own * n
    tokens, width = prefix_cache.shape
    suffix = suffix_cache.shape[1]
    slots = tokens + own * suffix
    rows = requests * heads
    mergers, _ = mergers_of(n)
    merge_heads = heads // mergers
    merge_rows = merge_heads * requests
    pack_rows = heads + max(16, heads // 2)
    vdim = w_uv.shape[2]
    columns = w_out.shape[1]
    share = requests // t
    bf, f32 = jnp.bfloat16, jnp.float32
    sizes = (n, t, own, heads, requests, tokens, suffix)
    vmem = pl.BlockSpec(memory_space=pltpu.VMEM)
    hbm = pl.BlockSpec(memory_space=pl.ANY)
    dma = pltpu.SemaphoreType.DMA
    return pl.pallas_call(
        functools.partial(kernel, sizes),
        out_shape=jax.ShapeDtypeStruct((share, columns), bf),
        in_specs=[hbm] * 10,
        out_specs=vmem,
        scratch_shapes=[
            pltpu.VMEM((own, heads, ROPE), bf),
            pltpu.VMEM((own, pack_rows, LANES), bf),
            pltpu.VMEM((requests, pack_rows, LANES), bf),
            pltpu.VMEM((rows, NOPE), f32),
            pltpu.VMEM((rows, ROPE), f32),
            pltpu.VMEM((rows, width), bf),
            pltpu.VMEM(w_uk.shape, bf),
            pltpu.VMEM(w_uv.shape, bf),
            pltpu.VMEM(w_out.shape, bf),
            pltpu.VMEM((width, slots), bf),
            pltpu.VMEM((requests, slots), f32),
            pltpu.VMEM((rows, slots), f32),
            pltpu.VMEM((rows, LANES), f32),
            pltpu.VMEM((rows, LANES), f32),
            pltpu.VMEM((rows, LAT), f32),
            pltpu.VMEM((mergers, merge_rows, vdim), bf),
            pltpu.VMEM((n, merge_rows, vdim), bf),
            pltpu.VMEM((mergers, 2, merge_rows), f32),
            pltpu.VMEM((n, 2, merge_rows), f32),
            pltpu.VMEM((LANES, LANES), f32),
            pltpu.VMEM((LANES, LANES), f32),
            pltpu.VMEM((mergers, requests, merge_heads * vdim), bf),
            pltpu.VMEM((t, share, columns), f32),
            pltpu.VMEM((t, share, columns), f32),
            pltpu.SMEM(block_table.shape, jnp.int32),
            pltpu.SMEM(prefix_len.shape, jnp.int32),
            pltpu.SMEM(suffix_len.shape, jnp.int32),
            dma((4 + own,)),
            dma((5,)),
            dma((n,)),
            dma(()),
            dma((mergers,)),
            dma(()),
            dma((mergers,)),
            dma(()),
            dma((n,)),
            dma((mergers,)),
            dma((t,)),
            dma((t,)),
        ],
        compiler_params=pltpu.CompilerParams(
            collective_id=0, has_side_effects=True, vmem_limit_bytes=50 * 1024 * 1024
        ),
    )(
        suffix_len,
        pltpu.with_memory_space_constraint(block_table, pltpu.HBM),
        pltpu.with_memory_space_constraint(prefix_len, pltpu.HBM),
        pltpu.with_memory_space_constraint(q_nope, pltpu.HBM),
        pltpu.with_memory_space_constraint(q_rope, pltpu.HBM),
        pltpu.with_memory_space_constraint(w_uk, pltpu.HBM),
        pltpu.with_memory_space_constraint(w_uv, pltpu.HBM),
        pltpu.with_memory_space_constraint(w_out, pltpu.HBM),
        pltpu.with_memory_space_constraint(prefix_cache.T, pltpu.HBM),
        pltpu.with_memory_space_constraint(jnp.swapaxes(suffix_cache, 1, 2), pltpu.HBM),
    )


def solution(mesh):
    placed = (
        P("ctx", "tp", None),
        P("ctx", "tp", None),
        P("tp", None, None),
        P("tp", None, None),
        P("tp", "ctx"),
        P("ctx", None),
        P("ctx"),
        P(),
        P("ctx", None, None),
        P("ctx"),
    )
    return jax.shard_map(
        functools.partial(on_device, mesh.shape["ctx"], mesh.shape["tp"]),
        mesh=mesh,
        in_specs=placed,
        out_specs=P("tp", "ctx"),
        check_vma=False,
    )
```

```python
import functools

import jax
import jax.numpy as jnp
from jax import lax
from jax.experimental import pallas as pl
from jax.experimental.pallas import tpu as pltpu
from jax.sharding import PartitionSpec as P

LAT = 512
ROPE = 64
NOPE = 128
BLOCK = 64
LANES = 128
MASKED = -1e30
FLOOR = -1e29
LOG2E = 1.4426950408889634
MESH = pl.DeviceIdType.MESH


def mergers_of(n):
    return (n // 2, n // 4) if n % 4 == 0 else (n, 0)


def flipped(index, k):
    bit = 1
    out = index
    while bit <= k:
        if k & bit:
            out = out + bit * (1 - 2 * lax.rem(index // bit, 2))
        bit *= 2
    return out


def kernel(
    sizes,
    suffix_len_hbm,
    table_hbm,
    prefix_len_hbm,
    q_nope_hbm,
    q_rope_hbm,
    w_uk_hbm,
    w_uv_hbm,
    w_out_hbm,
    prefix_hbm,
    suffix_hbm,
    out_ref,
    q_rope_ref,
    q_pack,
    q_all,
    qn_rows,
    qr_rows,
    query,
    w_uk,
    w_uv,
    w_out,
    cache,
    mask,
    scores,
    peak,
    mass,
    weighted,
    msg,
    got,
    stat_msg,
    stat_got,
    stat_rows,
    stat_columns,
    hv_all,
    part,
    part_got,
    table_ref,
    prefix_len_ref,
    suffix_len_ref,
    load_sem,
    small_sem,
    q_send,
    q_recv,
    m_send,
    m_recv,
    s_send,
    s_recv,
    h_send,
    h_recv,
    p_send,
    p_recv,
):
    n, t, own, heads, requests, tokens, suffix = sizes
    rows = requests * heads
    vdim = w_uv.shape[2]
    mergers, first = mergers_of(n)
    merge_heads = heads // mergers
    merge_rows = merge_heads * requests
    me = lax.axis_index("ctx")
    me_tp = lax.axis_index("tp")
    half_heads = heads // 2

    def ctx(index):
        return (index, me_tp)

    def copy_to(src, dst, send, recv, device):
        return pltpu.make_async_remote_copy(
            src_ref=src,
            dst_ref=dst,
            send_sem=send,
            recv_sem=recv,
            device_id=device,
            device_id_type=MESH,
        )

    smalls = [
        pltpu.make_async_copy(src, dst, small_sem.at[i])
        for i, (src, dst) in enumerate(
            (
                (q_nope_hbm, q_pack.at[:, pl.ds(0, heads)]),
                (q_rope_hbm, q_rope_ref),
                (table_hbm, table_ref),
                (prefix_len_hbm, prefix_len_ref),
                (suffix_len_hbm, suffix_len_ref),
            )
        )
    ]
    for small in smalls:
        small.start()
    loads = [
        pltpu.make_async_copy(w_uk_hbm, w_uk, load_sem.at[0]),
        pltpu.make_async_copy(prefix_hbm, cache.at[:, pl.ds(0, tokens)], load_sem.at[1]),
    ]
    for o in range(own):
        loads.append(
            pltpu.make_async_copy(
                suffix_hbm.at[o],
                cache.at[:, pl.ds(tokens + o * suffix, suffix)],
                load_sem.at[4 + o],
            )
        )
    uv_load = pltpu.make_async_copy(w_uv_hbm, w_uv, load_sem.at[2])
    out_load = pltpu.make_async_copy(w_out_hbm, w_out, load_sem.at[3])
    barrier = pltpu.get_barrier_semaphore()
    for k in reversed(range(1, n)):
        pl.semaphore_signal(barrier, inc=1, device_id=ctx(flipped(me, k)), device_id_type=MESH)
    for k in reversed(range(1, t)):
        pl.semaphore_signal(
            barrier, inc=1, device_id=(me, flipped(me_tp, k)), device_id_type=MESH
        )
    for small in smalls[:2]:
        small.wait()
    for o in range(own):
        rope = q_rope_ref[o]
        q_pack[o, heads : heads + half_heads, :] = jnp.concatenate(
            [rope[:half_heads], rope[half_heads:]], axis=1
        )
    for load in loads:
        load.start()
    uv_load.start()
    out_load.start()
    pl.semaphore_wait(barrier, n - 1 + t - 1)

    mine = pl.ds(me * own, own)
    q_copies = []
    for k in reversed(range(1, n)):
        copy = copy_to(q_pack, q_all.at[mine], q_send.at[k], q_recv, ctx(flipped(me, k)))
        copy.start()
        q_copies.append(copy)
    q_all[mine] = q_pack[...]
    for small in smalls[2:]:
        small.wait()

    stat_rows[...] = jnp.zeros_like(stat_rows)
    row = lax.broadcasted_iota(jnp.int32, (requests, LANES), 0)
    lane = lax.broadcasted_iota(jnp.int32, (requests, LANES), 1)
    limit = jnp.zeros((requests, LANES), jnp.int32)
    for r in range(requests):
        limit = jnp.where(row == r, prefix_len_ref[r], limit)
    per_tile = LANES // BLOCK
    for i in range(tokens // LANES):
        position = lane + table_ref[i * per_tile] * BLOCK
        for j in range(1, per_tile):
            moved = lane + (table_ref[i * per_tile + j] * BLOCK - j * BLOCK)
            position = jnp.where(lane >= j * BLOCK, moved, position)
        mask[:, i * LANES : (i + 1) * LANES] = jnp.where(position < limit, 0.0, MASKED)
    for o in range(own):
        for i in range(suffix // LANES):
            slot = lane + i * LANES
            start = tokens + o * suffix + i * LANES
            seen = (slot < suffix_len_ref[o]) & (row == me * own + o)
            mask[:, start : start + LANES] = jnp.where(seen, 0.0, MASKED)

    others = q_all.at[pl.ds(0, (n - 1) * own)]
    pltpu.make_async_copy(others, others, q_recv).wait()
    for r in range(requests):
        qn_rows[pl.ds(r, heads, stride=requests), :] = q_all[r, :heads, :].astype(jnp.float32)
        rope = q_all[r, heads : heads + half_heads, :].astype(jnp.float32)
        qr_rows[pl.ds(r, half_heads, stride=requests), :] = rope[:, :ROPE]
        qr_rows[pl.ds(half_heads * requests + r, half_heads, stride=requests), :] = rope[:, ROPE:]
    query[:, LAT:] = qr_rows[...].astype(jnp.bfloat16)
    loads[0].wait()
    latents = []
    for h in range(heads):
        q = qn_rows[h * requests : (h + 1) * requests, :]
        latents.append(
            jnp.dot(q.astype(jnp.bfloat16), w_uk[h], preferred_element_type=jnp.float32)
        )
    query[:, :LAT] = jnp.concatenate(latents, axis=0).astype(jnp.bfloat16)

    scale = LOG2E * (NOPE + ROPE) ** (-0.5)
    spans = [(0, tokens + own * suffix)]
    for load in loads[1:]:
        load.wait()
    uv_load.wait()
    block = rows // 2
    for b in range(2):
        at = slice(b * block, (b + 1) * block)
        tops = []
        for start, length in spans:
            s = jnp.dot(
                query[at, :], cache[:, start : start + length], preferred_element_type=jnp.float32
            )
            s = (s * scale).reshape(heads // 2, requests, length)
            s = (s + mask[:, start : start + length][None]).reshape(block, length)
            scores[at, start : start + length] = s
            tops += [s[:, j * LANES : (j + 1) * LANES] for j in range(length // LANES)]
        top = functools.reduce(jnp.maximum, tops)
        highest = jnp.maximum(jnp.max(top, axis=1, keepdims=True), FLOOR)
        peak[at, :] = jnp.broadcast_to(highest, (block, LANES))
    for i, (start, length) in enumerate(spans):
        p = jnp.exp2(scores[:, start : start + length] - peak[:, :1]).astype(jnp.bfloat16)
        wide = p.astype(jnp.float32)
        total = wide[:, :LANES]
        for j in range(1, length // LANES):
            total = total + wide[:, j * LANES : (j + 1) * LANES]
        mass[...] = total if i == 0 else mass[...] + total
        term = lax.dot_general(
            p,
            cache[:LAT, start : start + length],
            (((1,), (1,)), ((), ())),
            preferred_element_type=jnp.float32,
        )
        weighted[...] = term if i == 0 else weighted[...] + term
    half_lanes = LANES // 2
    folded = mass[...] + pltpu.roll(mass[...], half_lanes, 1)
    upper = lax.broadcasted_iota(jnp.int32, (rows, LANES), 1) >= half_lanes
    turned = jnp.transpose(jnp.where(upper, folded, peak[...]))
    mass_row = jnp.sum(turned[half_lanes:], axis=0, keepdims=True)
    stats = jnp.concatenate([turned[:1], mass_row], axis=0)
    for j in range(mergers):
        stat_msg[j] = stats[:, j * merge_rows : (j + 1) * merge_rows]

    nearest = (me // (n // 2)) * (mergers // 2) + lax.rem(me, mergers // 2)
    merging = jnp.logical_and(me >= first, me < first + mergers)
    order = [flipped(nearest, k) for k in range(mergers)]

    def stat_copy(k):
        j = order[k]
        return copy_to(stat_msg.at[j], stat_got.at[me], s_send.at[k], s_recv, ctx(first + j))

    def sum_copy(k):
        j = order[k]
        return copy_to(msg.at[j], got.at[me], m_send.at[k], m_recv, ctx(first + j))

    for k in reversed(range(1, mergers)):
        stat_copy(k).start()

    @pl.when(jnp.logical_not(merging))
    def _():
        stat_copy(0).start()

    for k in reversed(range(mergers)):
        j = order[k]
        parts = []
        for i in range(merge_heads):
            at = pl.multiple_of((j * merge_heads + i) * requests, requests)
            x = weighted[pl.ds(at, requests), :]
            high = x.astype(jnp.bfloat16).astype(jnp.float32)
            pieces = jnp.concatenate([high, x - high], axis=0).astype(jnp.bfloat16)
            y = jnp.dot(
                pieces, w_uv[j * merge_heads + i], preferred_element_type=jnp.float32
            )
            parts.append(y[:requests] + y[requests:])
        msg[j] = jnp.concatenate(parts, axis=0).astype(jnp.bfloat16)
        if k > 0:
            sum_copy(k).start()

    @pl.when(jnp.logical_not(merging))
    def _():
        sum_copy(0).start()

    def value_copy(k):
        at = hv_all.at[me - first]
        to = k - 1 + (k - 1 + n - me) // n
        return copy_to(at, at, h_send.at[k], h_recv.at[me - first], ctx(to))

    @pl.when(merging)
    def _():
        got[me] = msg[me - first]
        stat_got[me] = stat_msg[me - first]
        others = stat_got.at[pl.ds(0, n - 1)]
        pltpu.make_async_copy(others, others, s_recv).wait()
        tops = jnp.concatenate([stat_got[k][:1] for k in range(n)], axis=0)
        masses = jnp.concatenate([stat_got[k][1:] for k in range(n)], axis=0)
        share_of = jnp.exp2(tops - jnp.max(tops, axis=0, keepdims=True))
        whole = jnp.sum(share_of * masses, axis=0, keepdims=True)
        stat_rows[:n, :merge_rows] = share_of / whole
        stat_columns[...] = jnp.transpose(stat_rows[...])
        others = got.at[pl.ds(0, n - 1)]
        pltpu.make_async_copy(others, others, m_recv).wait()
        merged = None
        for k in range(n):
            term = stat_columns[:merge_rows, k : k + 1] * got[k].astype(jnp.float32)
            merged = term if merged is None else merged + term
        values = [merged[i * requests : (i + 1) * requests] for i in range(merge_heads)]
        hv_all[me - first] = jnp.concatenate(values, axis=1).astype(jnp.bfloat16)
        for k in range(1, n):
            value_copy(k).start()

    out_load.wait()
    depth = merge_heads * vdim
    total = None
    for k in range(mergers):
        j = order[k]

        def arrived():
            copy_to(
                hv_all.at[j], hv_all.at[j], h_send.at[0], h_recv.at[j], ctx(first + j)
            ).wait_recv()

        if k == 0:
            pl.when(jnp.logical_not(merging))(arrived)
        else:
            arrived()
        term = jnp.dot(
            hv_all[j],
            w_out[pl.ds(pl.multiple_of(j * depth, depth), depth), :],
            preferred_element_type=jnp.float32,
        )
        total = term if total is None else total + term
    share = requests // t
    for i in range(t):
        part[i] = total[i * share : (i + 1) * share]
    p_copies = []
    for k in reversed(range(1, t)):
        to = flipped(me_tp, k)
        copy = copy_to(part.at[to], part_got.at[k], p_send.at[k], p_recv, (me, to))
        copy.start()
        p_copies.append((k, copy))
    for copy in q_copies:
        copy.wait_send()
    for k in range(1, mergers):
        stat_copy(k).wait_send()
        sum_copy(k).wait_send()

    @pl.when(jnp.logical_not(merging))
    def _():
        stat_copy(0).wait_send()
        sum_copy(0).wait_send()

    @pl.when(merging)
    def _():
        for k in range(1, n):
            value_copy(k).wait_send()

    others = part_got.at[pl.ds(0, t - 1)]
    pltpu.make_async_copy(others, others, p_recv).wait()
    result = part[me_tp]
    for k in range(1, t):
        result = result + part_got[k]
    out_ref[...] = result.astype(jnp.bfloat16)
    for k, copy in p_copies:
        copy.wait_send()


def on_device(
    n,
    t,
    q_nope,
    q_rope,
    w_uk,
    w_uv,
    w_out,
    prefix_cache,
    block_table,
    prefix_len,
    suffix_cache,
    suffix_len,
):
    own, heads, _ = q_nope.shape
    requests = own * n
    tokens, width = prefix_cache.shape
    suffix = suffix_cache.shape[1]
    slots = tokens + own * suffix
    rows = requests * heads
    mergers, _ = mergers_of(n)
    merge_heads = heads // mergers
    merge_rows = merge_heads * requests
    pack_rows = heads + max(16, heads // 2)
    vdim = w_uv.shape[2]
    columns = w_out.shape[1]
    share = requests // t
    bf, f32 = jnp.bfloat16, jnp.float32
    sizes = (n, t, own, heads, requests, tokens, suffix)
    vmem = pl.BlockSpec(memory_space=pltpu.VMEM)
    hbm = pl.BlockSpec(memory_space=pl.ANY)
    dma = pltpu.SemaphoreType.DMA
    return pl.pallas_call(
        functools.partial(kernel, sizes),
        out_shape=jax.ShapeDtypeStruct((share, columns), bf),
        in_specs=[hbm] * 10,
        out_specs=vmem,
        scratch_shapes=[
            pltpu.VMEM((own, heads, ROPE), bf),
            pltpu.VMEM((own, pack_rows, LANES), bf),
            pltpu.VMEM((requests, pack_rows, LANES), bf),
            pltpu.VMEM((rows, NOPE), f32),
            pltpu.VMEM((rows, ROPE), f32),
            pltpu.VMEM((rows, width), bf),
            pltpu.VMEM(w_uk.shape, bf),
            pltpu.VMEM(w_uv.shape, bf),
            pltpu.VMEM(w_out.shape, bf),
            pltpu.VMEM((width, slots), bf),
            pltpu.VMEM((requests, slots), f32),
            pltpu.VMEM((rows, slots), f32),
            pltpu.VMEM((rows, LANES), f32),
            pltpu.VMEM((rows, LANES), f32),
            pltpu.VMEM((rows, LAT), f32),
            pltpu.VMEM((mergers, merge_rows, vdim), bf),
            pltpu.VMEM((n, merge_rows, vdim), bf),
            pltpu.VMEM((mergers, 2, merge_rows), f32),
            pltpu.VMEM((n, 2, merge_rows), f32),
            pltpu.VMEM((LANES, LANES), f32),
            pltpu.VMEM((LANES, LANES), f32),
            pltpu.VMEM((mergers, requests, merge_heads * vdim), bf),
            pltpu.VMEM((t, share, columns), f32),
            pltpu.VMEM((t, share, columns), f32),
            pltpu.SMEM(block_table.shape, jnp.int32),
            pltpu.SMEM(prefix_len.shape, jnp.int32),
            pltpu.SMEM(suffix_len.shape, jnp.int32),
            dma((4 + own,)),
            dma((5,)),
            dma((n,)),
            dma(()),
            dma((mergers,)),
            dma(()),
            dma((mergers,)),
            dma(()),
            dma((n,)),
            dma((mergers,)),
            dma((t,)),
            dma(()),
        ],
        compiler_params=pltpu.CompilerParams(
            collective_id=0, has_side_effects=True, vmem_limit_bytes=50 * 1024 * 1024
        ),
    )(
        suffix_len,
        pltpu.with_memory_space_constraint(block_table, pltpu.HBM),
        pltpu.with_memory_space_constraint(prefix_len, pltpu.HBM),
        pltpu.with_memory_space_constraint(q_nope, pltpu.HBM),
        pltpu.with_memory_space_constraint(q_rope, pltpu.HBM),
        pltpu.with_memory_space_constraint(w_uk, pltpu.HBM),
        pltpu.with_memory_space_constraint(w_uv, pltpu.HBM),
        pltpu.with_memory_space_constraint(w_out, pltpu.HBM),
        pltpu.with_memory_space_constraint(prefix_cache.T, pltpu.HBM),
        pltpu.with_memory_space_constraint(jnp.swapaxes(suffix_cache, 1, 2), pltpu.HBM),
    )


def solution(mesh):
    placed = (
        P("ctx", "tp", None),
        P("ctx", "tp", None),
        P("tp", None, None),
        P("tp", None, None),
        P("tp", "ctx"),
        P("ctx", None),
        P("ctx"),
        P(),
        P("ctx", None, None),
        P("ctx"),
    )
    return jax.shard_map(
        functools.partial(on_device, mesh.shape["ctx"], mesh.shape["tp"]),
        mesh=mesh,
        in_specs=placed,
        out_specs=P("tp", "ctx"),
        check_vma=False,
    )
```
